32 devices in a mesh: grp: 2 (over y), seq: 16 (over z, x, core).
Axes of the slice: x: 2, y: 2, z: 4, core: 2. Of those that a mesh axis runs over, the one named last changes fastest.
Arguments:
- ssd_inputs: bfloat16 [8192, 2048], P(('grp', 'seq')), parts along dimension 0
- gate_values: bfloat16 [8192, 2048], P(('grp', 'seq')), parts along dimension 0
- write_keys: bfloat16 [8192, 512], P(('grp', 'seq')), parts along dimension 0, may hold values from -1.796875 to 1.796875
- read_keys: bfloat16 [8192, 512], P(('grp', 'seq')), parts along dimension 0, may hold values from -1.796875 to 1.796875
- log_decay: float32 [8192, 64], P(('grp', 'seq')), parts along dimension 0, as said below
- transcript_len: int32 [8], P('grp'), parts along dimension 0, may hold values from 1 to 1536, 4096 in all
- norm_gain: float32 [2048], replicated, may hold values from 0.25 to 1.75
- probe_weights: bfloat16 [16, 8, 2048], P('seq'), may hold values from -0.125 to 0.125
- resp_rows: int32 [4096], P(('grp', 'seq')), parts along dimension 0, may hold values from 0 to 255, as said below
- probe_owner: int32 [4096, 1], P(('grp', 'seq')), parts along dimension 0, may hold values from 0 to 15; in each aligned block of 128 rows (0 to 127, 128 to 255, ...) at most 16 rows name the same one
Outputs:
- probe_out: float32 [4096, 8], P(('grp', 'seq')), parts along dimension 0
The draws below stay inside these ranges and needn't reach their ends.
There are 2 independent parts, one for each index of `grp`. The reference program is written for one: setup_inputs(seed, part) draws one part's arguments, and reference() takes and returns one part's arrays. A program takes and returns all parts, laid end to end along the dimension named above; an argument that names none is the same for every part. Nothing has to cross between parts.
Inputs may be any that keep to these rules, and one draw needn't show every extreme that they name: `transcript_len`: the transcripts lie end to end over the part's 4096 positions. `resp_rows`: each index of seq lists exactly 128 distinct positions of its own 256. `probe_owner`: among the 128 entries of one index of seq, no probe is named more than 16 times. `log_decay`: never positive.
All inputs are finite; a program needn't handle non-finite values.
Results may differ from the reference program's by a relative error of at most 0.0041.
Values may be sent and summed in bfloat16 or wider, within the bound.
A program may use at most 320 MiB of HBM per device.

```python
import math
import jax
import jax.numpy as jnp
import numpy as np
from jax import lax

HEADS = 64
HEAD_DIM = 32
STATE = 64
GROUPS = 8
STRETCH = 128
PROBE_OUT = 8
TRANSCRIPTS = 4
TOK_DEV = 256
RESP = 128
PART_POSITIONS = 4096
RESPONSES = 2048
PROBES = 16
CAP = 16
SPAN_MOST = 1536
N_SEQ = 16


def head_rates(key):
    random_key_sequence = jax.random.split(jax.random.fold_in(key, 11), 3)
    fast_share = 0.5
    fast_mask = jax.random.uniform(random_key_sequence[0], (HEADS,)) < fast_share
    fast_rate = 0.025 * jnp.exp(jax.random.uniform(random_key_sequence[1], (HEADS,), minval=-0.69, maxval=0.69))
    slow_rate = 0.1 / PART_POSITIONS * jnp.exp(jax.random.uniform(random_key_sequence[2], (HEADS,), minval=-0.69, maxval=0.69))
    return jnp.where(fast_mask, fast_rate, slow_rate)


def draw_log_decay(key, part):
    head_rate = head_rates(key)
    random_key_sequence = jax.random.split(jax.random.fold_in(key, 21), 4)
    blocks = PART_POSITIONS // TOK_DEV
    block_factor = jnp.exp(jax.random.uniform(random_key_sequence[0], (blocks, 1), minval=-0.69, maxval=0.69))
    rough_part = jax.random.uniform(random_key_sequence[1], (PART_POSITIONS, HEADS), minval=0.5, maxval=1.5)
    decay_rate_rows = jnp.repeat(block_factor, TOK_DEV, axis=0) * rough_part * head_rate[None, :]
    surge_row_list = jax.random.randint(random_key_sequence[2], (3,), 0, PART_POSITIONS)
    surge_depth = jax.random.uniform(random_key_sequence[3], (3,), minval=0.22, maxval=0.51)
    token_offsets = jnp.arange(PART_POSITIONS, dtype=jnp.int32)
    surge_portion = jnp.sum((token_offsets[:, None] == surge_row_list[None, :]).astype(jnp.float32) * surge_depth[None, :], axis=1)
    return -(decay_rate_rows + surge_portion[:, None])


def draw_ssd_inputs(key, part):
    head_rate = head_rates(key)
    col_scale = jnp.repeat(jnp.sqrt(2.0 * head_rate), HEAD_DIM)
    noise_key = jax.random.fold_in(key, 31)
    noise_part = jax.random.normal(noise_key, (PART_POSITIONS, HEADS * HEAD_DIM))
    return (noise_part * col_scale[None, :]).astype(jnp.bfloat16)


def draw_gate_values(key, part):
    random_key_sequence = jax.random.split(jax.random.fold_in(key, 41), 3)
    width = HEADS * HEAD_DIM
    col_scale = jnp.exp(jax.random.uniform(random_key_sequence[0], (1, width), minval=math.log(0.3), maxval=math.log(3.0)))
    row_scale = jnp.exp(jax.random.uniform(random_key_sequence[1], (PART_POSITIONS, 1), minval=math.log(0.3), maxval=math.log(3.0)))
    noise_part = jax.random.normal(random_key_sequence[2], (PART_POSITIONS, width))
    return (noise_part * col_scale * row_scale).astype(jnp.bfloat16)


def pick_rows(block_key):
    return jax.random.permutation(block_key, TOK_DEV)[:RESP]


def draw_resp_rows(key, part):
    blocks = PART_POSITIONS // TOK_DEV
    random_key_sequence = jax.random.split(jax.random.fold_in(key, 51), blocks)
    chosen = jax.vmap(pick_rows)(random_key_sequence)
    return chosen.reshape(-1).astype(jnp.int32)


def level_of(own_key, shape, shards, smallest, high):
    loudness = 1.0
    for dim, blocks in shards:
        steps = jax.random.uniform(jax.random.fold_in(jax.random.fold_in(own_key, 6), dim), (blocks,), jnp.float32, smallest / len(shards), high / len(shards))
        loudness = loudness * jnp.repeat(jnp.exp(steps), shape[dim] // blocks).reshape((-1,) + (1,) * (len(shape) - 1 - dim))
    return loudness


def split_up(amount, total, reach, slope):
    portions = [(1 << 20) // math.isqrt(standing ** slope) + 1 for standing in range(2, amount + 1)]
    rest, counts = total - reach - (amount - 1), [1] * (amount - 1)
    while rest > 0:
        movable = [i for i in range(amount - 1) if counts[i] < reach]
        whole, remaining = sum([portions[i] for i in movable]), rest
        for i in movable:
            extra = min(reach - counts[i], max(1, remaining * portions[i] // whole), rest)
            counts[i] = counts[i] + extra
            rest = rest - extra
    return np.array([reach] + counts)


def ragged_sizes(rng, amount, total, most, skew):
    if amount == 2:
        one = jax.random.randint(rng, (), max(1, total - most), min(most, total - 1) + 1)
        return jnp.stack([one, total - one])
    lengths = jnp.asarray(split_up(amount, total, most, skew), jnp.int32)
    pairs = (amount - 1) // 2
    donor, taker = lengths[1:1 + 2 * pairs:2], lengths[2:2 + 2 * pairs:2]
    slack = jnp.minimum(donor - 1, most - taker)
    passed = jax.random.randint(jax.random.fold_in(rng, 1), (pairs,), 0, 1 << 20) % (slack + 1)
    lengths = lengths.at[1:1 + 2 * pairs:2].set(donor - passed).at[2:2 + 2 * pairs:2].set(taker + passed)
    return lengths[jax.random.permutation(jax.random.fold_in(rng, 2), amount)]


def assign_block(stream_key, own, number, rows, amount, top, limit, slope):
    order = jax.random.permutation(stream_key, amount)
    crowded, ordinary = shares(amount, rows * top, limit, slope, True), shares(amount, rows * top, limit, slope, False)
    places = jnp.arange(amount)

    def named(sizes, rotation):
        used = int((sizes > 0).sum())
        fixed = max(1, used // 4)
        shifted = fixed + (places - fixed + rotation * (used - fixed)) % max(1, amount - fixed)
        return jnp.zeros((amount,), jnp.int32).at[order[jnp.where(places < fixed, places, shifted)]].set(jnp.asarray(sizes, jnp.int32))

    sizes = jnp.where(number % 4 == 0, named(crowded, number // 4), named(ordinary, number - number // 4 - 1))
    mixed = jax.random.permutation(jax.random.fold_in(own, 3), amount)
    source_of, taker = mixed[0:amount // 2 * 2:2], mixed[1:amount // 2 * 2:2]
    room = jnp.minimum(sizes[source_of] - 1, limit - sizes[taker]) // 2
    room = jnp.where((source_of == order[0]) | (taker == order[0]) | (sizes[taker] == 0), 0, jnp.maximum(room, 0))
    shifted = jax.random.randint(jax.random.fold_in(own, 4), (amount // 2,), 0, 1 << 20) % (room + 1)
    sizes = sizes.at[source_of].add(-shifted).at[taker].add(shifted)
    items = jnp.searchsorted(jnp.cumsum(sizes), jnp.arange(rows * top), side="right").astype(jnp.int32)
    listing = items.reshape(top, rows).T
    listing = listing[jax.random.permutation(jax.random.fold_in(own, 1), rows)]
    rotation = jax.random.randint(jax.random.fold_in(own, 2), (rows, 1), 0, top)
    return jnp.take_along_axis(listing, (jnp.arange(top)[None, :] + rotation) % top, axis=1)


def shares(number_of, total, bound, skew, full):
    weights = [(1 << 20) // math.isqrt(grade ** skew) + 1 for grade in range(1, number_of + 1)]
    largest = bound if full else min(bound, max(-(-total // number_of), total * weights[0] // sum(weights)))
    least = 1 if total - largest >= number_of - 1 else 0
    holding, rest = [largest] + [least] * (number_of - 1), total - largest - least * (number_of - 1)
    while rest > 0:
        candidates = [i for i in range(1, number_of) if holding[i] < largest] or [i for i in range(1, number_of) if holding[i] < bound]
        whole, remaining = sum([weights[i] for i in candidates]), rest
        for i in candidates:
            more = min(bound - holding[i], max(1, remaining * weights[i] // whole), rest)
            holding[i] = holding[i] + more
            rest = rest - more
    return np.array(holding)


def noise(key, dims, deviation, reach, shards=(), kind=jnp.bfloat16):
    result = deviation * jax.random.normal(key, dims, jnp.float32)
    if shards:
        result = result * level_of(key, dims, shards, -0.22, 0.18)
    return jnp.clip(result, -reach, reach).astype(kind)


def setup_inputs(seed: int = 0, part: int = 0) -> dict:
    seeds = jax.random.split(jax.random.key(seed), 11)
    part_keys = jax.random.split(jax.random.fold_in(seeds[10], part), 11)
    ssd_inputs = draw_ssd_inputs(jax.random.fold_in(jax.random.fold_in(seeds[10], part), 71), part)
    gate_values = draw_gate_values(jax.random.fold_in(jax.random.fold_in(seeds[10], part), 71), part)
    write_keys = noise(part_keys[2], (PART_POSITIONS, GROUPS * STATE), 0.3, 1.796875, ((0, 16),))
    read_keys = noise(part_keys[3], (PART_POSITIONS, GROUPS * STATE), 0.3, 1.796875, ((0, 16),))
    log_decay = draw_log_decay(jax.random.fold_in(jax.random.fold_in(seeds[10], part), 71), part)
    transcript_len = ragged_sizes(part_keys[5], TRANSCRIPTS, PART_POSITIONS, SPAN_MOST, 2).astype(jnp.int32)
    norm_gain = jnp.clip(1.0 + 0.15 * jax.random.normal(seeds[6], (HEADS * HEAD_DIM,), jnp.float32), 0.25, 1.75)
    probe_weights = noise(seeds[7], (PROBES, PROBE_OUT, HEADS * HEAD_DIM), (HEADS * HEAD_DIM) ** -0.5, 0.125, ((0, 16),))
    resp_rows = draw_resp_rows(jax.random.fold_in(jax.random.fold_in(seeds[10], part), 71), part)
    probe_owner_keys = jax.random.split(jax.random.fold_in(part_keys[9], 1), RESPONSES // RESP)
    probe_owner_turns = jax.random.permutation(jax.random.fold_in(part_keys[9], 3), RESPONSES // RESP)
    probe_owner = jax.vmap(lambda own, number: assign_block(jax.random.fold_in(part_keys[9], 2), own, number, RESP, PROBES, 1, CAP, 2))(probe_owner_keys, probe_owner_turns).reshape((RESPONSES, 1))
    return dict(ssd_inputs=ssd_inputs, gate_values=gate_values, write_keys=write_keys, read_keys=read_keys, log_decay=log_decay, transcript_len=transcript_len, norm_gain=norm_gain, probe_weights=probe_weights, resp_rows=resp_rows, probe_owner=probe_owner)


def transcript_of(transcript_len, token_offsets):
    span_ends = jnp.cumsum(transcript_len)
    return lax.optimization_barrier(jnp.sum((token_offsets[:, None] >= span_ends[None, :]).astype(jnp.int32), axis=1))

def stretch_output(values, read_rows, writes, decay_blk, docs_blk, prev_blk, carried_state):
    per_group = HEADS // GROUPS
    cum_decay = jnp.cumsum(decay_blk, axis=0)
    order = jnp.arange(STRETCH, dtype=jnp.int32)
    same_span = (docs_blk[:, None] == docs_blk[None, :]) & (order[:, None] >= order[None, :])
    read_f32 = read_rows.reshape(STRETCH, GROUPS, STATE).astype(jnp.float32)
    write_f32 = writes.reshape(STRETCH, GROUPS, STATE).astype(jnp.float32)
    keys_dot = jnp.einsum('tgn,sgn->gts', read_f32, write_f32)
    spread = cum_decay.T[:, :, None] - cum_decay.T[:, None, :]
    decay_mat = jnp.exp(jnp.where(same_span[None], spread, 0.0)) * same_span[None].astype(jnp.float32)
    weights = (keys_dot.reshape(GROUPS, 1, STRETCH, STRETCH) * decay_mat.reshape(GROUPS, per_group, STRETCH, STRETCH)).astype(jnp.bfloat16)
    value_f32 = values.reshape(STRETCH, GROUPS, per_group, HEAD_DIM).astype(jnp.float32)
    inner_part = jnp.einsum('ghts,sghp->tghp', weights.astype(jnp.float32), value_f32)
    carried = jnp.einsum('tgn,ghnp->tghp', read_f32, carried_state.reshape(GROUPS, per_group, STATE, HEAD_DIM), precision=lax.Precision.HIGHEST)
    row_scale = jnp.exp(cum_decay) * (docs_blk == prev_blk).astype(jnp.float32)[:, None]
    return (inner_part + carried * row_scale.reshape(STRETCH, GROUPS, per_group, 1)).reshape(STRETCH, HEADS * HEAD_DIM)

def stretch_state(values, writes, decay_blk, docs_blk, prev_blk):
    per_group = HEADS // GROUPS
    cum_decay = jnp.cumsum(decay_blk, axis=0)
    last_cum = cum_decay[-1]
    in_span = (docs_blk == docs_blk[-1]).astype(jnp.float32)
    factor = jnp.exp(last_cum[None, :] - cum_decay) * in_span[:, None]
    end_weights = (writes.reshape(STRETCH, GROUPS, 1, STATE).astype(jnp.float32) * factor.reshape(STRETCH, GROUPS, per_group, 1)).astype(jnp.bfloat16)
    value_f32 = values.reshape(STRETCH, GROUPS, per_group, HEAD_DIM).astype(jnp.float32)
    block_state = jnp.einsum('sghn,sghp->ghnp', end_weights.astype(jnp.float32), value_f32)
    keep_flag = (docs_blk[-1] == prev_blk).astype(jnp.float32)
    return (block_state.reshape(HEADS, STATE, HEAD_DIM), keep_flag * jnp.exp(last_cum))

def gate_norm(block_out, gates, norm_gain):
    gated = block_out * jax.nn.silu(gates.astype(jnp.float32))
    grouped = gated.reshape(gated.shape[0], GROUPS, -1)
    mean_square = lax.optimization_barrier(jnp.mean(grouped * grouped, axis=-1, keepdims=True))
    scaled = grouped / jnp.sqrt(mean_square + 1e-05)
    return (scaled.reshape(gated.shape[0], -1) * norm_gain).astype(jnp.bfloat16)

def reference(ssd_inputs, gate_values, write_keys, read_keys, log_decay, transcript_len, norm_gain, probe_weights, resp_rows, probe_owner):
    row_total = ssd_inputs.shape[0]
    block_count = row_total // STRETCH
    transcript = transcript_of(transcript_len, jnp.arange(row_total, dtype=jnp.int32))
    shaped = transcript.reshape(block_count, STRETCH)
    before = jnp.concatenate([jnp.full((1,), -1, jnp.int32), shaped[:-1, -1]])
    pieces = (ssd_inputs.reshape(block_count, STRETCH, -1), gate_values.reshape(block_count, STRETCH, -1), write_keys.reshape(block_count, STRETCH, -1), read_keys.reshape(block_count, STRETCH, -1), log_decay.reshape(block_count, STRETCH, -1), shaped, before)

    def scan_step(carried_state, piece):
        values, gates, writes, read_rows, decay_blk, docs_blk, prev_blk = piece
        block_out = stretch_output(values, read_rows, writes, decay_blk, docs_blk, prev_blk, carried_state)
        block_state, factor = stretch_state(values, writes, decay_blk, docs_blk, prev_blk)
        return (factor[:, None, None] * carried_state + block_state, gate_norm(block_out, gates, norm_gain))
    unused, normed = lax.scan(scan_step, jnp.zeros((HEADS, STATE, HEAD_DIM), jnp.float32), pieces)
    normed = normed.reshape(row_total, -1)
    owner_ids = probe_owner[:, 0].reshape(N_SEQ, RESP)
    row_index = resp_rows.reshape(N_SEQ, RESP) + (jnp.arange(N_SEQ, dtype=jnp.int32) * TOK_DEV)[:, None]

    def probe_block(piece):
        block_rows, block_owner = piece
        picked = jnp.take(normed, block_rows, axis=0).astype(jnp.float32)
        matrices = jnp.take(probe_weights, block_owner, axis=0).astype(jnp.float32)
        return jnp.einsum('rd,rod->ro', picked, matrices)
    probe_out = lax.map(probe_block, (row_index, owner_ids))
    return probe_out.reshape(N_SEQ * RESP, PROBE_OUT)
```

```python
import functools

import jax
import jax.numpy as jnp
from jax import lax
from jax.experimental import pallas as pl
from jax.experimental.pallas import tpu as pltpu
from jax.sharding import PartitionSpec as P

HEADS = 64
HEAD_DIM = 32
STATE = 64
GROUPS = 8
PROBE_OUT = 8
PER_GROUP = HEADS // GROUPS
WIDTH = PER_GROUP * HEAD_DIM
HALF = GROUPS // 2 * STATE
LOG2E = 1.4426950408889634
MESH = pl.DeviceIdType.MESH
F32, BF16, I32 = jnp.float32, jnp.bfloat16, jnp.int32


def dot(a, b):
    return jnp.dot(a, b, preferred_element_type=F32)


def dot_nt(a, b):
    return lax.dot_general(a, b, (((1,), (1,)), ((), ())), preferred_element_type=F32)


def each(start, stop, step):
    for g in range(start, stop):
        step(g)


def iota(shape, dim):
    return lax.broadcasted_iota(I32, shape, dim)


def pieces(x, count):
    parts = []
    for _ in range(count):
        part = x.astype(BF16)
        parts.append(part)
        x = x - part.astype(F32)
    return parts


CHUNK = 2
CHUNKS = GROUPS // 2 // CHUNK
ROWS = CHUNK * STATE


def kernel(
    n,
    steps,
    len_hbm,
    x_hbm,
    gate_hbm,
    write_hbm,
    read_hbm,
    decay_hbm,
    gain_hbm,
    probe_ref,
    rows_hbm,
    owner_hbm,
    out_ref,
    len_ref,
    x_ref,
    gate_ref,
    write_ref,
    read_ref,
    decay_ref,
    gain_ref,
    rows_ref,
    owner_ref,
    probes,
    state,
    inner,
    silu,
    dec,
    run_dec,
    run_e,
    run_w,
    half_send,
    half_recv,
    dec_recv,
    w_send,
    w_recv,
    d_send,
    d_recv,
    v_send,
    v_recv,
    entering,
    seen_ref,
    onehot_ref,
    cum_ref,
    cum_sel_ref,
    factor_ref,
    write_t_ref,
    read_sel_ref,
    row_parts_ref,
    owner_ref2,
    probe_sems,
    fwd_sems,
    share_sems,
    half_sems,
    v_sems,
    dec_sems,
    step_sems,
    local_sem,
    load_sems,
):
    tok = x_ref.shape[0]
    resp = rows_ref.shape[1]
    chips = n // 2
    tall = chips // 2
    me = lax.axis_index("seq")
    chip, core = me // 2, me % 2
    up, side = chip // 2, chip % 2
    sibling = {"seq": me + 1 - 2 * core}

    def device(c):
        return {"seq": 2 * c + core}

    beside = device(chip + 1 - 2 * side)

    def remote(src, dst, sems, where):
        return pltpu.make_async_remote_copy(
            src_ref=src,
            dst_ref=dst,
            send_sem=sems.at[0],
            recv_sem=sems.at[1],
            device_id=where,
            device_id_type=MESH,
        )

    loads = {}
    for k, (name, src, dst) in enumerate(
        [
            ("decay", decay_hbm, decay_ref),
            ("rows", rows_hbm, rows_ref),
            ("owner", owner_hbm, owner_ref),
            ("len", len_hbm, len_ref),
            ("write", write_hbm, write_ref),
            ("x", x_hbm, x_ref),
            ("read", read_hbm, read_ref),
            ("gate", gate_hbm, gate_ref),
            ("gain", gain_hbm, gain_ref),
        ]
    ):
        loads[name] = pltpu.make_async_copy(src, dst, load_sems.at[k])
        loads[name].start()
    own_slot = side * tall + up
    own_probe = pltpu.make_async_copy(probe_ref.at[0], probes.at[core, own_slot], local_sem)
    own_probe.start()

    barrier = pltpu.get_barrier_semaphore()
    pl.semaphore_signal(barrier, inc=1, device_id=sibling, device_id_type=MESH)
    for off in range(1, chips):
        pl.semaphore_signal(
            barrier, inc=1, device_id=device((chip + off) % chips), device_id_type=MESH
        )

    for name in ("decay", "rows", "owner", "len"):
        loads[name].wait()
    first = me * tok
    rows_row = rows_ref[...]
    s_row = iota((1, tok), 1)
    upto = jnp.concatenate(
        [
            (iota((tok, tok), 0) <= iota((tok, tok), 1)).astype(F32),
            (iota((tok, resp), 0) <= rows_row).astype(F32),
        ],
        axis=1,
    ).astype(BF16)
    sums = dot(jnp.concatenate(pieces(decay_ref[...], 3), axis=0), upto)
    sums = sums[:HEADS] + (sums[HEADS : 2 * HEADS] + sums[2 * HEADS :])
    cum = sums[:, :tok]
    cum_sel = sums[:, tok:].T
    last_cum = cum[:, tok - 1 : tok]

    def transcript(position):
        end, count = 0, jnp.zeros_like(position)
        for k in range(len_ref.shape[0]):
            end = end + len_ref[k]
            count = count + jnp.where(position >= end, 1, 0)
        return count

    docs = transcript(s_row + first)
    last_doc = transcript(jnp.full((1, 1), first + tok - 1, I32))
    prev_doc = transcript(jnp.full((1, 1), first - 1, I32))
    in_span = (docs == last_doc).astype(F32)
    keep = (last_doc == prev_doc).astype(F32)
    docs_sel = transcript(rows_row + first)

    eye = iota((resp, resp), 0) == iota((resp, resp), 1)

    def column(row):
        spread = jnp.broadcast_to(row.astype(F32), (resp, resp))
        return jnp.sum(jnp.where(eye, spread, 0.0), axis=1, keepdims=True)

    rows_col, docs_col, owner_col = column(rows_row), column(docs_sel), column(owner_ref[...])
    s_full = iota((resp, tok), 1).astype(F32)
    onehot_ref[...] = (s_full == rows_col).astype(F32).astype(BF16)
    seen_ref[...] = jnp.where((s_full <= rows_col) & (docs.astype(F32) == docs_col), 1.0, 0.0)
    for g in range(GROUPS):
        heads = slice(g * PER_GROUP, (g + 1) * PER_GROUP)
        cum_ref[g] = cum[heads] * LOG2E
        cum_sel_ref[g] = cum_sel[:, heads] * LOG2E
    row_scale = jnp.exp(cum_sel) * (docs_col == prev_doc.astype(F32)).astype(F32)
    row_parts_ref[...] = jnp.concatenate(pieces(row_scale, 2), axis=1)
    owner_ref2[...] = owner_col

    total = (keep * jnp.exp(last_cum)).T
    in_group = iota((GROUPS, HEADS), 1) // PER_GROUP == iota((GROUPS, HEADS), 0)
    by_group = jnp.where(in_group, total, 0.0)
    place = (iota((HEADS, WIDTH), 0) % PER_GROUP == iota((HEADS, WIDTH), 1) // HEAD_DIM)
    place = place.astype(F32).astype(BF16)
    spread = dot(jnp.concatenate(pieces(by_group, 3), axis=0), place)
    dec[...] = spread[:GROUPS] + (spread[GROUPS : 2 * GROUPS] + spread[2 * GROUPS :])

    loads["write"].wait()
    factor = jnp.exp(last_cum - cum) * in_span
    for g in range(GROUPS):
        factor_ref[g] = factor[g * PER_GROUP : (g + 1) * PER_GROUP]
    write_t_ref[...] = write_ref[...].astype(F32).T.astype(BF16)
    lane_head = iota((1, WIDTH), 1) // HEAD_DIM

    def columns(g):
        return pl.ds(pl.multiple_of(g * WIDTH, WIDTH), WIDTH)

    def pair_of(g):
        return pl.ds(pl.multiple_of(g // 2 * 2 * STATE, 2 * STATE), 2 * STATE)

    def state_of(g):
        group = pl.ds(pl.multiple_of(g * STATE, STATE), STATE)
        keys = write_t_ref[group, :].astype(F32)
        by_head = factor_ref[g]
        scaled = [(keys * by_head[j : j + 1]).astype(BF16) for j in range(PER_GROUP)]
        product = dot(jnp.concatenate(scaled, axis=0), x_ref[:, columns(g)])
        kept = product[:STATE]
        for j in range(1, PER_GROUP):
            kept = jnp.where(lane_head == j, product[j * STATE : (j + 1) * STATE], kept)
        state[group, :] = kept

    def rows_of(j):
        return pl.ds(j * ROWS, ROWS)

    def half_rows(k, j):
        return pl.ds(pl.multiple_of(k * HALF + j * ROWS, ROWS), ROWS)

    def dec_rows(ref, k, j):
        rows = [
            jnp.broadcast_to(ref[pl.ds(k * (GROUPS // 2) + j * CHUNK + i, 1), :], (STATE, WIDTH))
            for i in range(CHUNK)
        ]
        return jnp.concatenate(rows, axis=0)

    half_copies = [
        remote(half_send.at[rows_of(j)], half_recv.at[rows_of(j)], half_sems.at[j], sibling)
        for j in range(CHUNKS)
    ]
    dec_copy = remote(dec, dec_recv, dec_sems, sibling)

    loads["x"].wait()
    for k in range(GROUPS // 2):
        state_of((1 - core) * (GROUPS // 2) + k)
    half_send[...] = state[pl.ds(pl.multiple_of((1 - core) * HALF, HALF), HALF), :].astype(BF16)
    pl.semaphore_wait(barrier, chips)
    dec_copy.start()
    for copy in half_copies:
        copy.start()
    probe_copies = [
        remote(
            probe_ref.at[0],
            probes.at[core, own_slot],
            probe_sems.at[off],
            device((up + off) % tall * 2 + side),
        )
        for off in range(1, tall)
    ]
    probe_copies.append(
        remote(probe_ref.at[0], probes.at[core, own_slot], probe_sems.at[0], beside)
    )
    for copy in probe_copies:
        copy.start()
    for k in range(GROUPS // 2):
        state_of(core * (GROUPS // 2) + k)

    loads["read"].wait()
    read_sel_ref[...] = dot(onehot_ref[...], read_ref[...]).astype(BF16)
    lane = iota((1, 2 * STATE), 1)

    def read_of(g):
        both = read_sel_ref[:, pair_of(g)]
        return jnp.where((lane // STATE) == g % 2, both.astype(F32), 0.0).astype(BF16)

    def inner_of(g):
        keys_dot = jnp.where(seen_ref[...] != 0.0, dot(read_of(g), write_t_ref[pair_of(g), :]), 0.0)
        sums_t, sums_s = cum_sel_ref[g], cum_ref[g]
        values = x_ref[:, columns(g)]
        for j in range(PER_GROUP):
            gap = sums_t[:, j : j + 1] - sums_s[j : j + 1]
            weight = keys_dot * jnp.exp2(jnp.minimum(gap, 0.0))
            product = dot(weight.astype(BF16), values)
            kept = product if j == 0 else jnp.where(lane_head == j, product, kept)
        inner[:, columns(g)] = kept

    def silu_of(g):
        gates = dot(onehot_ref[...], gate_ref[:, columns(g)])
        silu[:, columns(g)] = gates / (1.0 + jnp.exp(-gates))

    is_first = core == 0

    def w_copy(i, j):
        return remote(
            w_send.at[i, rows_of(j)],
            w_recv.at[i, rows_of(j)],
            step_sems.at[i, j],
            device((chip + (1 << i)) % chips),
        )

    def d_copy(i):
        return remote(
            d_send.at[i], d_recv.at[i], step_sems.at[i, CHUNKS], device((chip + (1 << i)) % chips)
        )

    run_e[...] = jnp.zeros_like(run_e)
    inner_of(0)
    dec_copy.wait_recv()
    run_dec[0] = jnp.ones_like(dec)
    run_dec[1] = dec[...] * dec_recv[...]
    d_send[0] = run_dec[1]

    @pl.when(chip + 1 < chips)
    def _():
        d_copy(0).start()

    for j in range(CHUNKS):
        half_copies[j].wait_recv()
        own, other = state[half_rows(core, j), :], half_recv[rows_of(j), :].astype(F32)
        later_dec = jnp.where(is_first, dec_rows(dec_recv, core, j), dec_rows(dec, core, j))
        merged = later_dec * jnp.where(is_first, own, other) + jnp.where(is_first, other, own)
        run_w[rows_of(j), :] = merged
        w_send[0, rows_of(j), :] = merged.astype(BF16)

        @pl.when(chip + 1 < chips)
        def _():
            w_copy(0, j).start()

    def column_slots(s):
        return pl.ds(s * tall, tall)

    def share(k, s):
        part = probes.at[k, column_slots(s)]
        return remote(part, part, share_sems.at[s], sibling)

    forwards = []
    for off in range(1, tall):
        slot = side * tall + (up + tall - off) % tall
        part = probes.at[core, slot]
        forwards.append(remote(part, part, fwd_sems.at[off], beside))

    def forward_probes():
        for off in range(1, tall):
            came = probes.at[core, side * tall + (up + tall - off) % tall]
            remote(came, came, probe_sems.at[off], beside).wait_recv()
            forwards[off - 1].start()
        own_probe.wait()
        share(core, side).start()

    def share_probes():
        other = probes.at[core, (1 - side) * tall + up]
        remote(other, other, probe_sems.at[0], beside).wait_recv()
        for off in range(1, tall):
            came = probes.at[core, (1 - side) * tall + (up + tall - off) % tall]
            remote(came, came, fwd_sems.at[off], beside).wait_recv()
        share(core, 1 - side).start()

    per_step = (GROUPS - 2) // steps
    done = 1
    loads["gate"].wait()
    for i in range(steps):
        reach = 1 << i
        more = i + 1 < steps
        each(done, done + per_step, inner_of)
        each(GROUPS * i // steps, GROUPS * (i + 1) // steps, silu_of)
        done += per_step
        if not more:
            each(done, GROUPS, inner_of)

        @pl.when(chip >= reach)
        def _():
            d_copy(i).wait_recv()

        if more:

            @pl.when(chip >= reach)
            def _():
                d_send[i + 1] = run_dec[1] * d_recv[i]

            @pl.when(chip < reach)
            def _():
                d_send[i + 1] = run_dec[1]

            @pl.when(chip + 2 * reach < chips)
            def _():
                d_copy(i + 1).start()

        for j in range(CHUNKS):

            @pl.when(chip >= reach)
            def _():
                w_copy(i, j).wait_recv()
                came = w_recv[i, rows_of(j), :].astype(F32)
                before = dec_rows(run_dec.at[0], core, j)
                run_e[rows_of(j), :] = run_e[rows_of(j), :] + before * came
                if more:
                    through = dec_rows(run_dec.at[1], core, j)
                    run_w[rows_of(j), :] = run_w[rows_of(j), :] + through * came

            if more:
                w_send[i + 1, rows_of(j), :] = run_w[rows_of(j), :].astype(BF16)

                @pl.when(chip + 2 * reach < chips)
                def _():
                    w_copy(i + 1, j).start()

            if i == 0 and j == 0:
                forward_probes()

        if more:

            @pl.when(chip >= reach)
            def _():
                run_dec[0] = run_dec[0] * d_recv[i]
                run_dec[1] = d_send[i + 1]


    v_copies = []
    for j in range(CHUNKS):
        enter_chip = run_e[rows_of(j), :]
        own, other = state[half_rows(core, j), :], half_recv[rows_of(j), :].astype(F32)
        mine = jnp.where(is_first, enter_chip, dec_rows(dec_recv, core, j) * enter_chip + other)
        theirs = jnp.where(is_first, dec_rows(dec, core, j) * enter_chip + own, enter_chip)
        v_send[rows_of(j), :] = theirs.astype(BF16)
        v_copies.append(
            remote(v_send.at[rows_of(j)], v_recv.at[rows_of(j)], v_sems.at[j], sibling)
        )
        v_copies[j].start()
        entering[half_rows(core, j), :] = mine.astype(BF16)

    share_probes()
    loads["gain"].wait()
    share(1 - core, side).wait_recv()
    share(1 - core, 1 - side).wait_recv()

    def readout(g, scores):
        heads = iota((2 * HEADS, WIDTH), 0) % HEADS
        spread = heads == g * PER_GROUP + iota((2 * HEADS, WIDTH), 1) // HEAD_DIM
        scale = dot(row_parts_ref[...], spread.astype(F32).astype(BF16))
        out = inner[:, columns(g)] + scale * dot(read_of(g), entering[pair_of(g), :])
        gated = out * silu[:, columns(g)]
        mean = jnp.sum(gated * gated, axis=1, keepdims=True) * (1.0 / WIDTH)
        normed = gated / jnp.sqrt(mean + 1e-05) * gain_ref[:, columns(g)]
        matrix = probes[:, :, :, columns(g)].astype(F32).reshape(n * PROBE_OUT, WIDTH)
        return scores + dot_nt(normed.astype(BF16), matrix.astype(BF16))

    scores = jnp.zeros((resp, n * PROBE_OUT), F32)
    for k in range(GROUPS // 2):
        scores = readout(core * (GROUPS // 2) + k, scores)
    for j in range(CHUNKS):
        v_copies[j].wait_recv()
        entering[half_rows(1 - core, j), :] = v_recv[rows_of(j), :]
    for k in range(GROUPS // 2):
        scores = readout((1 - core) * (GROUPS // 2) + k, scores)

    slot = iota((1, n * PROBE_OUT), 1) // PROBE_OUT
    at = slot % chips
    probe = (at % tall * 2 + at // tall) * 2 + slot // chips
    asked = jnp.where(probe.astype(F32) == owner_ref2[...], scores, 0.0)
    fold = iota((PROBE_OUT, n * PROBE_OUT), 1) % PROBE_OUT == iota((PROBE_OUT, n * PROBE_OUT), 0)
    fold = fold.astype(F32).astype(BF16)
    folded = [dot_nt(fold, part) for part in pieces(asked, 3)]
    out_ref[...] = folded[0] + (folded[1] + folded[2])

    for i in range(steps):

        @pl.when(chip + (1 << i) < chips)
        def _():
            d_copy(i).wait_send()
            for j in range(CHUNKS):
                w_copy(i, j).wait_send()

    for copy in probe_copies + forwards + half_copies + v_copies:
        copy.wait_send()
    dec_copy.wait_send()
    share(core, 0).wait_send()
    share(core, 1).wait_send()


def body(
    ssd_inputs,
    gate_values,
    write_keys,
    read_keys,
    log_decay,
    transcript_len,
    norm_gain,
    probe_weights,
    resp_rows,
    probe_owner,
):
    n = lax.axis_size("seq")
    chips = n // 2
    resp, tok = resp_rows.shape[0], ssd_inputs.shape[0]
    back = -(-(-(-3 * n // 8)) // 2)
    steps = back.bit_length()
    vmem = pl.BlockSpec(memory_space=pltpu.VMEM)
    return pl.pallas_call(
        functools.partial(kernel, n, steps),
        out_shape=pltpu.VMEM((PROBE_OUT, resp), F32),
        in_specs=[pl.BlockSpec(memory_space=pl.ANY)] * 10,
        out_specs=vmem,
        scratch_shapes=[
            pltpu.SMEM(transcript_len.shape, I32),
            pltpu.VMEM(ssd_inputs.shape, BF16),
            pltpu.VMEM(gate_values.shape, BF16),
            pltpu.VMEM(write_keys.shape, BF16),
            pltpu.VMEM(read_keys.shape, BF16),
            pltpu.VMEM((HEADS, tok), F32),
            pltpu.VMEM((1, HEADS * HEAD_DIM), F32),
            pltpu.VMEM((1, resp), I32),
            pltpu.VMEM((1, resp), I32),
            pltpu.VMEM((2, chips, PROBE_OUT, HEADS * HEAD_DIM), BF16),
            pltpu.VMEM((GROUPS * STATE, WIDTH), F32),
            pltpu.VMEM((resp, HEADS * HEAD_DIM), F32),
            pltpu.VMEM((resp, HEADS * HEAD_DIM), F32),
            pltpu.VMEM((GROUPS, WIDTH), F32),
            pltpu.VMEM((2, GROUPS, WIDTH), F32),
            pltpu.VMEM((HALF, WIDTH), F32),
            pltpu.VMEM((HALF, WIDTH), F32),
            pltpu.VMEM((HALF, WIDTH), BF16),
            pltpu.VMEM((HALF, WIDTH), BF16),
            pltpu.VMEM((GROUPS, WIDTH), F32),
            pltpu.VMEM((steps, HALF, WIDTH), BF16),
            pltpu.VMEM((steps, HALF, WIDTH), BF16),
            pltpu.VMEM((steps, GROUPS, WIDTH), F32),
            pltpu.VMEM((steps, GROUPS, WIDTH), F32),
            pltpu.VMEM((HALF, WIDTH), BF16),
            pltpu.VMEM((HALF, WIDTH), BF16),
            pltpu.VMEM((GROUPS * STATE, WIDTH), BF16),
            pltpu.VMEM((resp, tok), F32),
            pltpu.VMEM((resp, tok), BF16),
            pltpu.VMEM((GROUPS, PER_GROUP, tok), F32),
            pltpu.VMEM((GROUPS, resp, PER_GROUP), F32),
            pltpu.VMEM((GROUPS, PER_GROUP, tok), F32),
            pltpu.VMEM((GROUPS * STATE, tok), BF16),
            pltpu.VMEM((resp, GROUPS * STATE), BF16),
            pltpu.VMEM((resp, 2 * HEADS), BF16),
            pltpu.VMEM((resp, 1), F32),
            pltpu.SemaphoreType.DMA((chips // 2, 2)),
            pltpu.SemaphoreType.DMA((chips // 2, 2)),
            pltpu.SemaphoreType.DMA((2, 2)),
            pltpu.SemaphoreType.DMA((CHUNKS, 2)),
            pltpu.SemaphoreType.DMA((CHUNKS, 2)),
            pltpu.SemaphoreType.DMA((2,)),
            pltpu.SemaphoreType.DMA((steps, CHUNKS + 1, 2)),
            pltpu.SemaphoreType.DMA,
            pltpu.SemaphoreType.DMA((9,)),
        ],
        compiler_params=pltpu.CompilerParams(
            collective_id=0, has_side_effects=True, vmem_limit_bytes=60000 * 1024
        ),
        name="ssd_probe",
    )(
        transcript_len,
        ssd_inputs,
        gate_values,
        write_keys,
        read_keys,
        log_decay.T,
        norm_gain[None, :],
        probe_weights,
        resp_rows[None, :],
        probe_owner.T,
    ).T


def solution(mesh):
    return jax.shard_map(
        body,
        mesh=mesh,
        in_specs=(
            P(("grp", "seq"), None),
            P(("grp", "seq"), None),
            P(("grp", "seq"), None),
            P(("grp", "seq"), None),
            P(("grp", "seq"), None),
            P("grp"),
            P(),
            P("seq", None, None),
            P(("grp", "seq")),
            P(("grp", "seq"), None),
        ),
        out_specs=P(("grp", "seq"), None),
        check_vma=False,
    )
```
